512 devices in a mesh: dev: 32 (over y_hi, z), ha: 2 (over y_lo), col: 8 (over x, core).
Axes of the slice: x: 4, y: 8 (y_hi: 4, y_lo: 2; y = y_hi * 2 + y_lo), z: 8, core: 2. Of those that a mesh axis runs over, the one named last changes fastest.
Arguments:
- features: bfloat16 [128, 128, 32, 128], P('col', 'dev', 'ha'), may hold values from -6 to 6
- kernel: bfloat16 [3, 3, 3, 128, 128], P(None, None, None, 'col'), may hold values from -0.109375 to 0.109375
- channel_bias: float32 [128], P('col'), may hold values from -3 to 3
Outputs:
- activated: bfloat16 [128, 128, 32, 128], P('col', 'dev', 'ha')
The draws below stay inside these ranges and needn't reach their ends.
All inputs are finite; a program needn't handle non-finite values.
Results may differ from the reference program's by a relative error of at most 0.005.
Values may be sent and summed in bfloat16 or wider, within the bound.
A program may use at most 64 MiB of HBM per device.

```python
import jax
import jax.numpy as jnp
from jax import lax

CIN = 128
COUT = 128
WIDTH = 128
DEPTH = 128
HEIGHT = 32


def shard_levels(key, dims, shards, low, high):
    factor_of, own = 1.0, jax.random.fold_in(key, 6)
    for dim, shards_of in shards:
        heights = jnp.exp(jax.random.uniform(jax.random.fold_in(own, dim), (shards_of,), jnp.float32, low / len(shards), high / len(shards)))
        factor_of = factor_of * jnp.repeat(heights, dims[dim] // shards_of).reshape([-1 if axis == dim else 1 for axis in range(len(dims))])
    return factor_of


def noise(rng, shape, scale, limit, cuts=(), kind=jnp.bfloat16):
    level = shard_levels(rng, shape, cuts, -0.22, 0.18) if cuts else 1.0
    drawn = jax.random.normal(rng, shape, jnp.float32) * scale * level
    return jnp.minimum(jnp.maximum(drawn, -limit), limit).astype(kind)


def setup_inputs(seed: int = 0) -> dict:
    key_list = jax.random.split(jax.random.key(seed), 4)
    return {
        "features": noise(key_list[0], (CIN, DEPTH, HEIGHT, WIDTH), 1.0, 6.0, ((0, 8), (1, 32), (2, 2))),
        "kernel": noise(key_list[1], (3, 3, 3, COUT, CIN), (27 * CIN) ** -0.5, 0.109375, ((3, 8),)),
        "channel_bias": noise(key_list[2], (COUT,), 0.5, 3.0, ((0, 8),), jnp.float32),
    }


def reference(features, kernel, channel_bias):
    inputs = features.astype(jnp.float32)[None]
    weights = jnp.transpose(kernel.astype(jnp.float32), (3, 4, 0, 1, 2))
    summed = lax.conv_general_dilated(inputs, weights, (1, 1, 1), ((1, 1), (1, 1), (1, 1)), dimension_numbers=("NCDHW", "OIDHW", "NCDHW"), precision=lax.Precision.HIGHEST)[0]
    summed = summed + channel_bias.astype(jnp.float32)[:, None, None, None]
    return jnp.where(summed >= 0, summed, 0.3 * summed).astype(jnp.bfloat16)
```

```python
import jax
import jax.numpy as jnp
from jax import lax
from jax.experimental import pallas as pl
from jax.experimental.pallas import tpu as pltpu
from jax.sharding import PartitionSpec as P

MESH = pl.DeviceIdType.MESH

ORDER = (0, 1, 6, 2, 3, 4, 5)
PLANE = {0: 1, 1: 2, 2: 3, 3: 4, 4: 0, 5: 5}
RELAY_RIGHT = (0, 2, 4)


def kernel(x_ref, k_ref, b_ref, o_ref, g, wb, acc, local_sem, hs, hr, ls, lr, rs, rr, xs, xr, ps, pr):
    dev, ha, col = lax.axis_index("dev"), lax.axis_index("ha"), lax.axis_index("col")
    devs = lax.axis_size("dev")
    chip, core = col // 2, lax.rem(col, 2)
    right = 2 * lax.rem(chip + 1, 4) + core
    left = 2 * lax.rem(chip + 3, 4) + core
    partner = 2 * chip + 1 - core
    up, down = lax.rem(dev + 1, devs), lax.rem(dev + devs - 1, devs)
    other = 1 - ha

    barrier = pltpu.get_barrier_semaphore()
    for target in (
        (dev, ha, right), (dev, ha, left), (dev, ha, partner), (up, ha, col), (down, ha, col),
        (dev, other, col), (up, other, col), (down, other, col),
    ):
        pl.semaphore_signal(barrier, inc=1, device_id=target, device_id_type=MESH)

    def slot(of_chip):
        return pl.ds(pl.multiple_of(core * 64 + of_chip * 16, 16), 16)

    mine = slot(chip)
    halo_row = 17 * other

    local = pltpu.make_async_copy(x_ref, g.at[1:5, 1:17, mine], local_sem)
    local.start()
    g[:, pl.ds(17 * ha, 1)] = jnp.zeros((6, 1, 128, 128), jnp.bfloat16)
    pl.semaphore_wait(barrier, 8)

    def remote(src, dst, send, recv, target):
        return pltpu.make_async_remote_copy(
            src_ref=src, dst_ref=dst, send_sem=send, recv_sem=recv,
            device_id=target, device_id_type=MESH,
        )

    edge = 15 * other
    halos = [
        remote(x_ref.at[3], g.at[0, 1:17, mine], hs.at[0], hr.at[0], (up, ha, col)),
        remote(x_ref.at[0], g.at[5, 1:17, mine], hs.at[1], hr.at[1], (down, ha, col)),
        remote(x_ref.at[:, edge], g.at[1:5, 17 * ha, mine], hs.at[2], hr.at[2], (dev, other, col)),
        remote(x_ref.at[3, edge], g.at[0, 17 * ha, mine], hs.at[3], hr.at[3], (up, other, col)),
        remote(x_ref.at[0, edge], g.at[5, 17 * ha, mine], hs.at[4], hr.at[4], (down, other, col)),
    ]
    for i in (2, 3, 4, 0, 1):
        halos[i].start()

    def part(unit, channels):
        if unit == 6:
            return g.at[:, halo_row, channels]
        return g.at[PLANE[unit], 1:17, channels]

    sends = []

    def own_source(unit):
        return x_ref.at[unit] if unit < 4 else part(unit, mine)

    def send_own(unit):
        if unit == 4:
            halos[0].wait_recv()
        if unit == 5:
            halos[1].wait_recv()
        if unit == 6:
            for i in (2, 3, 4):
                halos[i].wait_recv()
        for target, send, recv in ((right, ls, lr), (left, rs, rr)):
            copy = remote(own_source(unit), part(unit, mine), send.at[unit], recv.at[unit], (dev, ha, target))
            copy.start()
            sends.append(copy)

    def arrival(unit, channels, send, recv):
        return remote(part(unit, channels), part(unit, channels), send.at[unit], recv.at[unit], (dev, ha, partner))

    from_left = slot(lax.rem(chip + 3, 4))
    from_right = slot(lax.rem(chip + 1, 4))
    across = slot(lax.rem(chip + 2, 4))

    def relay(unit):
        arrival(unit, from_left, ls, lr).wait_recv()
        arrival(unit, from_right, rs, rr).wait_recv()
        channels, target = (from_left, right) if unit in RELAY_RIGHT else (from_right, left)
        copy = remote(part(unit, channels), part(unit, channels), xs.at[unit], xr.at[unit], (dev, ha, target))
        copy.start()
        sends.append(copy)

    my_half = pl.ds(pl.multiple_of(core * 64, 64), 64)
    its_half = pl.ds(pl.multiple_of((1 - core) * 64, 64), 64)

    def forward(unit):
        arrival(unit, across, xs, xr).wait_recv()
        copy = remote(part(unit, my_half), part(unit, my_half), ps.at[unit], pr.at[unit], (dev, ha, partner))
        copy.start()
        sends.append(copy)

    send_own(ORDER[0])
    send_own(ORDER[1])

    row = lax.broadcasted_iota(jnp.int32, (128, 128), 0)
    column = lax.broadcasted_iota(jnp.int32, (128, 128), 1)
    place = (row // 16 % 2) * 64 + (row // 32) * 16 + row % 16
    permutation = jnp.where(place == column, 1.0, 0.0).astype(jnp.bfloat16)
    for a in range(3):
        for b in range(3):
            taps = k_ref[a, b].reshape(48, 128)
            taps = jnp.dot(taps, permutation, preferred_element_type=jnp.float32)
            wb[a * 48 : a * 48 + 48, b * 128 : b * 128 + 128] = taps.astype(jnp.bfloat16)
    eye = lax.broadcasted_iota(jnp.int32, (16, 16), 0) == lax.broadcasted_iota(jnp.int32, (16, 16), 1)
    bias = jnp.sum(jnp.where(eye, b_ref[...], 0.0), axis=1, keepdims=True)

    first = {0: True, 1: True, 2: True, 3: True}

    def compute(plane):
        taps = [a for a in range(3) if 0 <= plane - a < 4]
        low, high = taps[0] * 48, taps[-1] * 48 + 48
        fresh = {a: first[plane - a] for a in taps}
        for a in taps:
            first[plane - a] = False

        def pair(j, carry):
            cells = jnp.concatenate(
                [g[plane, pl.ds(2 * j, 3)].reshape(384, 128), g[plane, pl.ds(2 * j + 1, 3)].reshape(384, 128)],
                axis=1,
            )
            out = jnp.dot(wb[low:high, :], cells, preferred_element_type=jnp.float32)
            for a in taps:
                value = out[a * 48 - low : a * 48 - low + 48]
                if fresh[a]:
                    acc[plane - a, j] = value
                else:
                    acc[plane - a, j] += value
            return carry

        lax.fori_loop(0, 8, pair, 0, unroll=2)

    lane = lax.broadcasted_iota(jnp.int32, (16, 128), 1)

    def finish(d):
        def pair(j, carry):
            for half in range(2):
                lanes = slice(half * 128, half * 128 + 128)
                before = pltpu.roll(acc[d, j, 0:16, lanes], 1, 1)
                after = pltpu.roll(acc[d, j, 32:48, lanes], 127, 1)
                total = acc[d, j, 16:32, lanes] + bias
                total += jnp.where(lane == 0, 0.0, before) + jnp.where(lane == 127, 0.0, after)
                o_ref[d, 2 * j + half] = jnp.where(total >= 0, total, 0.3 * total).astype(jnp.bfloat16)
            return carry

        lax.fori_loop(0, 8, pair, 0, unroll=2)

    waiting = []
    done = []
    steps = len(ORDER)
    for step in range(steps + 2):
        if step < steps:
            relay(ORDER[step])
        if step + 2 < steps:
            send_own(ORDER[step + 2])
        if 1 <= step <= steps:
            if step == 1:
                local.wait()
            forward(ORDER[step - 1])
        if step >= 2:
            unit = ORDER[step - 2]
            arrival(unit, its_half, ps, pr).wait_recv()
            done.append(unit)
            if unit != 6:
                waiting.append(PLANE[unit])
            if 6 in done:
                for plane in waiting:
                    if plane == 0:
                        pl.when(dev > 0)(lambda: compute(0))
                    elif plane == 5:
                        pl.when(dev < devs - 1)(lambda: compute(5))
                    else:
                        compute(plane)
                    if plane == 3:
                        finish(1)
                    if plane == 4:
                        finish(2)
                    if plane == 0:
                        finish(0)
                    if plane == 5:
                        finish(3)
                waiting = []
    for copy in halos + sends:
        copy.wait_send()


def per_device(features, weights, channel_bias):
    rows = jnp.transpose(features, (1, 2, 0, 3))
    dma = pltpu.SemaphoreType.DMA
    out = pl.pallas_call(
        kernel,
        out_shape=jax.ShapeDtypeStruct((4, 16, 16, 128), jnp.bfloat16),
        in_specs=[pl.BlockSpec(memory_space=pltpu.VMEM)] * 3,
        out_specs=pl.BlockSpec(memory_space=pltpu.VMEM),
        scratch_shapes=[
            pltpu.VMEM((6, 18, 128, 128), jnp.bfloat16),
            pltpu.VMEM((144, 384), jnp.bfloat16),
            pltpu.VMEM((4, 8, 48, 256), jnp.float32),
            dma(()),
            dma((5,)), dma((5,)),
            dma((7,)), dma((7,)), dma((7,)), dma((7,)),
            dma((7,)), dma((7,)), dma((7,)), dma((7,)),
        ],
        compiler_params=pltpu.CompilerParams(collective_id=0, has_side_effects=True),
    )(rows, weights, channel_bias[None, :])
    return jnp.transpose(out, (2, 0, 1, 3))


def solution(mesh):
    in_specs = (P("col", "dev", "ha", None), P(None, None, None, "col", None), P("col"))
    out_specs = P("col", "dev", "ha", None)
    return jax.shard_map(
        per_device, mesh=mesh, in_specs=in_specs, out_specs=out_specs, check_vma=False
    )
```

```python
import jax
import jax.numpy as jnp
from jax import lax
from jax.experimental import pallas as pl
from jax.experimental.pallas import tpu as pltpu
from jax.sharding import PartitionSpec as P

MESH = pl.DeviceIdType.MESH

ORDER = (0, 3, 1, 2, 6)
TAIL = (4, 5)
PLANE = {0: 1, 1: 2, 2: 3, 3: 4, 4: 0, 5: 5}
RELAY_RIGHT = (0, 1, 6)


def kernel(x_ref, k_hbm, b_hbm, o_hbm, g, wb, acc, k_ref, b_ref, o_ref, local_sem, os, hs, hr, ls, lr, rs, rr, xs, xr, ps, pr, zs, zr):
    dev, ha, col = lax.axis_index("dev"), lax.axis_index("ha"), lax.axis_index("col")
    devs = lax.axis_size("dev")
    chip, core = col // 2, lax.rem(col, 2)
    right = 2 * lax.rem(chip + 1, 4) + core
    left = 2 * lax.rem(chip + 3, 4) + core
    partner = 2 * chip + 1 - core
    up, down = lax.rem(dev + 1, devs), lax.rem(dev + devs - 1, devs)
    other = 1 - ha

    barrier = pltpu.get_barrier_semaphore()
    has_up, has_down = dev < devs - 1, dev > 0

    def greet(*targets):
        for target in targets:
            pl.semaphore_signal(barrier, inc=1, device_id=target, device_id_type=MESH)

    greet((dev, ha, right), (dev, ha, left), (dev, ha, partner), (dev, other, col))
    pl.when(has_up)(lambda: greet((up, ha, col), (up, other, col)))
    pl.when(has_down)(lambda: greet((down, ha, col), (down, other, col)))

    mine = chip
    halo_row = 17 * other

    local = pltpu.make_async_copy(x_ref, g.at[mine, core, 1:5, 1:17], local_sem.at[0])
    local.start()
    parameters = [
        pltpu.make_async_copy(k_hbm, k_ref, local_sem.at[1]),
        pltpu.make_async_copy(b_hbm, b_ref, local_sem.at[2]),
    ]
    for copy in parameters:
        copy.start()
    g[:, :, :, pl.ds(17 * ha, 1)] = jnp.zeros((4, 2, 6, 1, 16, 128), jnp.bfloat16)

    @pl.when(jnp.logical_not(has_down))
    def _():
        g[mine, core, 0, halo_row] = jnp.zeros((16, 128), jnp.bfloat16)

    @pl.when(jnp.logical_not(has_up))
    def _():
        g[mine, core, 5, halo_row] = jnp.zeros((16, 128), jnp.bfloat16)

    pl.semaphore_wait(barrier, 4 + 2 * has_up.astype(jnp.int32) + 2 * has_down.astype(jnp.int32))

    def remote(src, dst, send, recv, target):
        return pltpu.make_async_remote_copy(
            src_ref=src, dst_ref=dst, send_sem=send, recv_sem=recv,
            device_id=target, device_id_type=MESH,
        )

    edge = 15 * other
    halos = [
        remote(x_ref.at[3], g.at[mine, core, 0, 1:17], hs.at[0], hr.at[0], (up, ha, col)),
        remote(x_ref.at[0], g.at[mine, core, 5, 1:17], hs.at[1], hr.at[1], (down, ha, col)),
        remote(x_ref.at[:, edge], g.at[mine, core, 1:5, 17 * ha], hs.at[2], hr.at[2], (dev, other, col)),
        remote(x_ref.at[3, edge], g.at[mine, core, 0, 17 * ha], hs.at[3], hr.at[3], (up, other, col)),
        remote(x_ref.at[0, edge], g.at[mine, core, 5, 17 * ha], hs.at[4], hr.at[4], (down, other, col)),
    ]
    def part(unit, chips, side=core):
        if unit == 6:
            return g.at[chips, side, :, halo_row]
        return g.at[chips, side, PLANE[unit], 1:17]

    to = {0: has_up, 1: has_down, 2: None, 3: has_up, 4: has_down}
    come = {0: has_down, 1: has_up, 2: None, 3: has_down, 4: has_up}
    exists = {4: has_down, 5: has_up}

    def when(condition, act):
        if condition is None:
            act()
        else:
            pl.when(condition)(act)

    sends = []

    def own_source(unit):
        return x_ref.at[unit] if unit < 4 else part(unit, mine)

    def send(unit, target, send_sems, recv_sems):
        copy = remote(own_source(unit), part(unit, mine), send_sems.at[unit], recv_sems.at[unit], (dev, ha, target))
        when(exists.get(unit), copy.start)
        sends.append((exists.get(unit), copy))

    def send_own(unit):
        if unit == 6:
            for i in (2, 3, 4):
                when(come[i], halos[i].wait_recv)
        if unit in (4, 5):
            when(come[unit - 4], halos[unit - 4].wait_recv)
        if unit != 5:
            send(unit, right, ls, lr)
        if unit != 4:
            send(unit, left, rs, rr)

    def arrival(unit, chips, send, recv, side=core):
        return remote(part(unit, chips, side), part(unit, chips, side), send.at[unit], recv.at[unit], (dev, ha, partner))

    from_left = lax.rem(chip + 3, 4)
    from_right = lax.rem(chip + 1, 4)
    across = lax.rem(chip + 2, 4)

    def relay(unit):
        arrival(unit, from_left, ls, lr).wait_recv()
        arrival(unit, from_right, rs, rr).wait_recv()
        chips, target = (from_left, right) if unit in RELAY_RIGHT else (from_right, left)
        copy = remote(part(unit, chips), part(unit, chips), xs.at[unit], xr.at[unit], (dev, ha, target))
        copy.start()
        sends.append((None, copy))
        if unit == 0:
            when(has_down, to_depth[0].start)
        if unit == 3:
            when(has_up, to_depth[2].start)

    def depth(chips, halo, index):
        plane, target = (4, up) if halo == 0 else (1, down)
        return remote(
            g.at[chips, core, plane, 1:17], g.at[chips, core, halo, 1:17], zs.at[index], zr.at[index], (target, ha, col)
        )

    to_depth = [depth(from_left, 5, 0), depth(across, 5, 1), depth(from_right, 0, 2), depth(across, 0, 3)]
    every = pl.ds(0, 4)

    def forward(unit):
        def whole():
            if unit == 4:
                arrival(unit, from_left, ls, lr).wait_recv()
                to_depth[2].wait_recv()
                to_depth[3].wait_recv()
            elif unit == 5:
                arrival(unit, from_right, rs, rr).wait_recv()
                to_depth[0].wait_recv()
                to_depth[1].wait_recv()
            else:
                arrival(unit, across, xs, xr).wait_recv()

        copy = remote(part(unit, every), part(unit, every), ps.at[unit], pr.at[unit], (dev, ha, partner))
        when(exists.get(unit), whole)
        when(exists.get(unit), copy.start)
        sends.append((exists.get(unit), copy))
        if unit == 0:
            when(has_down, to_depth[1].start)
        if unit == 3:
            when(has_up, to_depth[3].start)

    send_own(ORDER[0])
    for i in (0, 1, 2, 3, 4):
        when(to[i], halos[i].start)
    send_own(ORDER[1])

    for copy in parameters:
        copy.wait()
    for a in range(3):
        for b in range(3):
            wb[a * 48 : a * 48 + 48, b * 128 : b * 128 + 128] = k_ref[a, b].reshape(48, 128)
    eye = lax.broadcasted_iota(jnp.int32, (16, 16), 0) == lax.broadcasted_iota(jnp.int32, (16, 16), 1)
    bias = jnp.sum(jnp.where(eye, b_ref[...], 0.0), axis=1, keepdims=True)

    seen = set()

    def compute(plane, pairs):
        taps = [a for a in range(3) if 0 <= plane - a < 4]
        low, high = taps[0] * 48, taps[-1] * 48 + 48
        fresh = {a: (plane - a, pairs) not in seen and pairs != "all" for a in taps}
        seen.update((plane - a, pairs) for a in taps)

        def pair(j, carry):
            rows = [g[:, :, plane, 2 * j + i].reshape(128, 128) for i in range(4)]
            cells = jnp.concatenate([jnp.concatenate(rows[i : i + 2], axis=1) for i in range(3)], axis=0)
            out = jnp.dot(wb[low:high, :], cells, preferred_element_type=jnp.float32)
            for a in taps:
                value = out[a * 48 - low : a * 48 - low + 48]
                if fresh[a]:
                    acc[plane - a, j] = value
                else:
                    acc[plane - a, j] += value
            return carry

        if pairs == "inner":
            lax.fori_loop(0, 7, lambda i, carry: pair(ha + i, carry), 0, unroll=7)
        elif pairs == "edge":
            pair(7 * other, 0)
        else:
            lax.fori_loop(0, 8, pair, 0, unroll=4)

    lane = lax.broadcasted_iota(jnp.int32, (16, 128), 1)

    def finish(d):
        def pair(j, carry):
            for half in range(2):
                lanes = slice(half * 128, half * 128 + 128)
                before = pltpu.roll(acc[d, j, 0:16, lanes], 1, 1)
                after = pltpu.roll(acc[d, j, 32:48, lanes], 127, 1)
                total = acc[d, j, 16:32, lanes] + bias
                total += jnp.where(lane == 0, 0.0, before) + jnp.where(lane == 127, 0.0, after)
                o_ref[d, 2 * j + half] = jnp.where(total >= 0, total, 0.3 * total).astype(jnp.bfloat16)
            return carry

        lax.fori_loop(0, 8, pair, 0, unroll=4)
        results[d].start()

    results = [pltpu.make_async_copy(o_ref.at[d], o_hbm.at[d], os.at[d]) for d in range(4)]
    queue = ORDER + TAIL
    steps = len(queue)
    for step in range(steps + 2):
        if step < len(ORDER):
            relay(queue[step])
        if step + 2 < steps:
            send_own(queue[step + 2])
        if 1 <= step <= steps:
            if step == 1:
                local.wait()
            forward(queue[step - 1])
        if step >= 2:
            unit = queue[step - 2]
            when(exists.get(unit), arrival(unit, every, ps, pr, 1 - core).wait_recv)
            if unit < 4:
                compute(PLANE[unit], "inner")
            elif unit == 6:
                for own in ORDER[:4]:
                    compute(PLANE[own], "edge")
                finish(1)
                finish(2)
            else:
                when(exists[unit], lambda: compute(PLANE[unit], "all"))
                finish(0 if unit == 4 else 3)
    for i in range(5):
        when(to[i], halos[i].wait_send)
    for i in range(4):
        when(has_down if i < 2 else has_up, to_depth[i].wait_send)
    for condition, copy in sends:
        when(condition, copy.wait_send)
    for copy in results:
        copy.wait()


def per_device(features, weights, channel_bias):
    rows = jnp.transpose(features, (1, 2, 0, 3))
    dma = pltpu.SemaphoreType.DMA
    out = pl.pallas_call(
        kernel,
        out_shape=jax.ShapeDtypeStruct((4, 16, 16, 128), jnp.bfloat16),
        in_specs=[pl.BlockSpec(memory_space=pl.ANY)] * 3,
        out_specs=pl.BlockSpec(memory_space=pl.ANY),
        scratch_shapes=[
            pltpu.VMEM((4, 2, 6, 18, 16, 128), jnp.bfloat16),
            pltpu.VMEM((144, 384), jnp.bfloat16),
            pltpu.VMEM((4, 8, 48, 256), jnp.float32),
            pltpu.VMEM((3, 3, 3, 16, 128), jnp.bfloat16),
            pltpu.VMEM((1, 16), jnp.float32),
            pltpu.VMEM((4, 16, 16, 128), jnp.bfloat16),
            dma((3,)), dma((4,)),
            dma((5,)), dma((5,)),
            dma((7,)), dma((7,)), dma((7,)), dma((7,)),
            dma((7,)), dma((7,)), dma((7,)), dma((7,)),
            dma((4,)), dma((4,)),
        ],
        compiler_params=pltpu.CompilerParams(collective_id=0, has_side_effects=True),
    )(rows, weights, channel_bias[None, :])
    return jnp.transpose(out, (2, 0, 1, 3))


def solution(mesh):
    in_specs = (P("col", "dev", "ha", None), P(None, None, None, "col", None), P("col"))
    out_specs = P("col", "dev", "ha", None)
    return jax.shard_map(
        per_device, mesh=mesh, in_specs=in_specs, out_specs=out_specs, check_vma=False
    )
```

```python
import jax
import jax.numpy as jnp
from jax import lax
from jax.experimental import pallas as pl
from jax.experimental.pallas import tpu as pltpu
from jax.sharding import PartitionSpec as P

MESH = pl.DeviceIdType.MESH

ORDER = (3, 0, 1, 2, 6)
TAIL = (4, 5)
LATE_STEP = 2
PLANE = {0: 1, 1: 2, 2: 3, 3: 4, 4: 0, 5: 5}
RELAY_RIGHT = (0, 1, 6)


def kernel(x_ref, k_hbm, b_hbm, o_hbm, g, wb, acc, k_ref, b_ref, o_ref, local_sem, os, ready, hs, hr, ls, lr, rs, rr, xs, xr, ps, pr, zs, zr):
    dev, ha, col = lax.axis_index("dev"), lax.axis_index("ha"), lax.axis_index("col")
    devs = lax.axis_size("dev")
    chip, core = col // 2, lax.rem(col, 2)
    right = 2 * lax.rem(chip + 1, 4) + core
    left = 2 * lax.rem(chip + 3, 4) + core
    partner = 2 * chip + 1 - core
    up, down = lax.rem(dev + 1, devs), lax.rem(dev + devs - 1, devs)
    other = 1 - ha

    barrier = pltpu.get_barrier_semaphore()
    has_up, has_down = dev < devs - 1, dev > 0
    late = jnp.logical_and(has_down, lax.rem(dev, 8) == 0)
    early = jnp.logical_and(has_up, lax.rem(dev, 8) == 7)
    greets_up = jnp.logical_and(has_up, jnp.logical_not(early))
    prompt = jnp.logical_and(has_down, jnp.logical_not(late))

    def greet(*targets):
        for target in targets:
            pl.semaphore_signal(barrier, inc=1, device_id=target, device_id_type=MESH)

    greet((dev, ha, right), (dev, ha, left), (dev, ha, partner), (dev, other, col))
    pl.when(greets_up)(lambda: greet((up, ha, col), (up, other, col)))
    pl.when(has_down)(lambda: greet((down, ha, col), (down, other, col)))

    mine = chip
    halo_row = 17 * other

    local = pltpu.make_async_copy(x_ref, g.at[mine, core, 1:5, 1:17], local_sem.at[0])
    local.start()
    parameters = [
        pltpu.make_async_copy(k_hbm, k_ref, local_sem.at[1]),
        pltpu.make_async_copy(b_hbm, b_ref, local_sem.at[2]),
    ]
    for copy in parameters:
        copy.start()
    g[:, :, :, pl.ds(17 * ha, 1)] = jnp.zeros((4, 2, 6, 1, 16, 128), jnp.bfloat16)

    @pl.when(jnp.logical_not(has_down))
    def _():
        g[mine, core, 0, halo_row] = jnp.zeros((16, 128), jnp.bfloat16)

    @pl.when(jnp.logical_not(has_up))
    def _():
        g[mine, core, 5, halo_row] = jnp.zeros((16, 128), jnp.bfloat16)

    pl.semaphore_wait(barrier, 4 + 2 * has_up.astype(jnp.int32) + 2 * prompt.astype(jnp.int32))

    @pl.when(early)
    def _():
        for target in ((up, ha, col), (up, other, col)):
            pl.semaphore_signal(ready, inc=1, device_id=target, device_id_type=MESH)

    def remote(src, dst, send, recv, target):
        return pltpu.make_async_remote_copy(
            src_ref=src, dst_ref=dst, send_sem=send, recv_sem=recv,
            device_id=target, device_id_type=MESH,
        )

    edge = 15 * other
    halos = [
        remote(x_ref.at[3], g.at[mine, core, 0, 1:17], hs.at[0], hr.at[0], (up, ha, col)),
        remote(x_ref.at[0], g.at[mine, core, 5, 1:17], hs.at[1], hr.at[1], (down, ha, col)),
        remote(x_ref.at[:, edge], g.at[mine, core, 1:5, 17 * ha], hs.at[2], hr.at[2], (dev, other, col)),
        remote(x_ref.at[3, edge], g.at[mine, core, 0, 17 * ha], hs.at[3], hr.at[3], (up, other, col)),
        remote(x_ref.at[0, edge], g.at[mine, core, 5, 17 * ha], hs.at[4], hr.at[4], (down, other, col)),
    ]
    def part(unit, chips, side=core):
        if unit == 6:
            return g.at[chips, side, :, halo_row]
        return g.at[chips, side, PLANE[unit], 1:17]

    to = {0: has_up, 1: has_down, 2: None, 3: has_up, 4: has_down}
    come = {0: has_down, 1: has_up, 2: None, 3: has_down, 4: has_up}
    exists = {4: has_down, 5: has_up}

    def when(condition, act):
        if condition is None:
            act()
        else:
            pl.when(condition)(act)

    sends = []

    def own_source(unit):
        return x_ref.at[unit] if unit < 4 else part(unit, mine)

    def send(unit, target, send_sems, recv_sems):
        copy = remote(own_source(unit), part(unit, mine), send_sems.at[unit], recv_sems.at[unit], (dev, ha, target))
        when(exists.get(unit), copy.start)
        sends.append((exists.get(unit), copy))

    def send_own(unit):
        if unit == 6:
            for i in (2, 3, 4):
                when(come[i], halos[i].wait_recv)
        if unit in (4, 5):
            when(come[unit - 4], halos[unit - 4].wait_recv)
        if unit != 5:
            send(unit, right, ls, lr)
        if unit != 4:
            send(unit, left, rs, rr)

    def arrival(unit, chips, send, recv, side=core):
        return remote(part(unit, chips, side), part(unit, chips, side), send.at[unit], recv.at[unit], (dev, ha, partner))

    from_left = lax.rem(chip + 3, 4)
    from_right = lax.rem(chip + 1, 4)
    across = lax.rem(chip + 2, 4)

    def relay(unit):
        arrival(unit, from_left, ls, lr).wait_recv()
        arrival(unit, from_right, rs, rr).wait_recv()
        chips, target = (from_left, right) if unit in RELAY_RIGHT else (from_right, left)
        copy = remote(part(unit, chips), part(unit, chips), xs.at[unit], xr.at[unit], (dev, ha, target))
        copy.start()
        sends.append((None, copy))
        if unit == 0:
            when(prompt, to_depth[0].start)
        if unit == 3:
            when(has_up, to_depth[2].start)

    def depth(chips, halo, index):
        plane, target = (4, up) if halo == 0 else (1, down)
        return remote(
            g.at[chips, core, plane, 1:17], g.at[chips, core, halo, 1:17], zs.at[index], zr.at[index], (target, ha, col)
        )

    to_depth = [depth(from_left, 5, 0), depth(across, 5, 1), depth(from_right, 0, 2), depth(across, 0, 3)]
    every = pl.ds(0, 4)

    def forward(unit):
        def whole():
            if unit == 4:
                arrival(unit, from_left, ls, lr).wait_recv()
                to_depth[2].wait_recv()
                to_depth[3].wait_recv()
            elif unit == 5:
                arrival(unit, from_right, rs, rr).wait_recv()
                to_depth[0].wait_recv()
                to_depth[1].wait_recv()
            else:
                arrival(unit, across, xs, xr).wait_recv()

        copy = remote(part(unit, every), part(unit, every), ps.at[unit], pr.at[unit], (dev, ha, partner))
        when(exists.get(unit), whole)
        when(exists.get(unit), copy.start)
        sends.append((exists.get(unit), copy))
        if unit == 0:
            when(prompt, to_depth[1].start)
        if unit == 3:
            when(has_up, to_depth[3].start)

    send_own(ORDER[0])
    for i in (0, 1, 2, 3, 4):
        when(prompt if i in (1, 4) else to[i], halos[i].start)
    send_own(ORDER[1])

    for copy in parameters:
        copy.wait()
    for a in range(3):
        for b in range(3):
            wb[a * 48 : a * 48 + 48, b * 128 : b * 128 + 128] = k_ref[a, b].reshape(48, 128)
    eye = lax.broadcasted_iota(jnp.int32, (16, 16), 0) == lax.broadcasted_iota(jnp.int32, (16, 16), 1)
    bias = jnp.sum(jnp.where(eye, b_ref[...], 0.0), axis=1, keepdims=True)

    seen = set()

    def compute(plane, pairs):
        taps = [a for a in range(3) if 0 <= plane - a < 4]
        low, high = taps[0] * 48, taps[-1] * 48 + 48
        fresh = {a: (plane - a, pairs) not in seen and pairs != "all" for a in taps}
        seen.update((plane - a, pairs) for a in taps)

        def pair(j, carry):
            rows = [g[:, :, plane, 2 * j + i].reshape(128, 128) for i in range(4)]
            cells = jnp.concatenate([jnp.concatenate(rows[i : i + 2], axis=1) for i in range(3)], axis=0)
            out = jnp.dot(wb[low:high, :], cells, preferred_element_type=jnp.float32)
            for a in taps:
                value = out[a * 48 - low : a * 48 - low + 48]
                if fresh[a]:
                    acc[plane - a, j] = value
                else:
                    acc[plane - a, j] += value
            return carry

        if pairs == "inner":
            lax.fori_loop(0, 7, lambda i, carry: pair(ha + i, carry), 0, unroll=7)
        elif pairs == "edge":
            pair(7 * other, 0)
        else:
            lax.fori_loop(0, 8, pair, 0, unroll=4)

    lane = lax.broadcasted_iota(jnp.int32, (16, 128), 1)

    def finish(d):
        def pair(j, carry):
            for half in range(2):
                lanes = slice(half * 128, half * 128 + 128)
                before = pltpu.roll(acc[d, j, 0:16, lanes], 1, 1)
                after = pltpu.roll(acc[d, j, 32:48, lanes], 127, 1)
                total = acc[d, j, 16:32, lanes] + bias
                total += jnp.where(lane == 0, 0.0, before) + jnp.where(lane == 127, 0.0, after)
                o_ref[d, 2 * j + half] = jnp.where(total >= 0, total, 0.3 * total).astype(jnp.bfloat16)
            return carry

        lax.fori_loop(0, 8, pair, 0, unroll=4)
        results[d].start()

    results = [pltpu.make_async_copy(o_ref.at[d], o_hbm.at[d], os.at[d]) for d in range(4)]
    queue = ORDER + TAIL
    steps = len(queue)
    for step in range(steps + 2):
        if step < len(ORDER):
            relay(queue[step])
        if step + 2 < steps:
            send_own(queue[step + 2])
        if 1 <= step <= steps:
            if step == 1:
                local.wait()
            forward(queue[step - 1])
        if step == LATE_STEP:

            @pl.when(late)
            def _():
                pl.semaphore_wait(ready, 2)
                for copy in (halos[4], halos[1], to_depth[0], to_depth[1]):
                    copy.start()

        if step >= 2:
            unit = queue[step - 2]
            when(exists.get(unit), arrival(unit, every, ps, pr, 1 - core).wait_recv)
            if unit < 4:
                compute(PLANE[unit], "inner")
            elif unit == 6:
                for own in ORDER[:4]:
                    compute(PLANE[own], "edge")
                finish(1)
                finish(2)
            else:
                when(exists[unit], lambda: compute(PLANE[unit], "all"))
                finish(0 if unit == 4 else 3)
    for i in range(5):
        when(to[i], halos[i].wait_send)
    for i in range(4):
        when(has_down if i < 2 else has_up, to_depth[i].wait_send)
    for condition, copy in sends:
        when(condition, copy.wait_send)
    for copy in results:
        copy.wait()


def per_device(features, weights, channel_bias):
    rows = jnp.transpose(features, (1, 2, 0, 3))
    dma = pltpu.SemaphoreType.DMA
    out = pl.pallas_call(
        kernel,
        out_shape=jax.ShapeDtypeStruct((4, 16, 16, 128), jnp.bfloat16),
        in_specs=[pl.BlockSpec(memory_space=pl.ANY)] * 3,
        out_specs=pl.BlockSpec(memory_space=pl.ANY),
        scratch_shapes=[
            pltpu.VMEM((4, 2, 6, 18, 16, 128), jnp.bfloat16),
            pltpu.VMEM((144, 384), jnp.bfloat16),
            pltpu.VMEM((4, 8, 48, 256), jnp.float32),
            pltpu.VMEM((3, 3, 3, 16, 128), jnp.bfloat16),
            pltpu.VMEM((1, 16), jnp.float32),
            pltpu.VMEM((4, 16, 16, 128), jnp.bfloat16),
            dma((3,)), dma((4,)), pltpu.SemaphoreType.REGULAR,
            dma((5,)), dma((5,)),
            dma((7,)), dma((7,)), dma((7,)), dma((7,)),
            dma((7,)), dma((7,)), dma((7,)), dma((7,)),
            dma((4,)), dma((4,)),
        ],
        compiler_params=pltpu.CompilerParams(collective_id=0, has_side_effects=True),
    )(rows, weights, channel_bias[None, :])
    return jnp.transpose(out, (2, 0, 1, 3))


def solution(mesh):
    in_specs = (P("col", "dev", "ha", None), P(None, None, None, "col", None), P("col"))
    out_specs = P("col", "dev", "ha", None)
    return jax.shard_map(
        per_device, mesh=mesh, in_specs=in_specs, out_specs=out_specs, check_vma=False
    )
```

```python
import jax
import jax.numpy as jnp
from jax import lax
from jax.experimental import pallas as pl
from jax.experimental.pallas import tpu as pltpu
from jax.sharding import PartitionSpec as P

MESH = pl.DeviceIdType.MESH

ORDER = (3, 0, 1, 2, 6)
TAIL = (4, 5)
LATE_STEP = 2
PLANE = {0: 1, 1: 2, 2: 3, 3: 4, 4: 0, 5: 5}
RELAY_RIGHT = (0, 1, 6)


def kernel(x_hbm, k_hbm, b_hbm, o_hbm, g, wb, acc, k_ref, b_ref, o_ref, x_in, x_ref, local_sem, os, ins, ready, hs, hr, ls, lr, rs, rr, xs, xr, ps, pr, zs, zr):
    dev, ha, col = lax.axis_index("dev"), lax.axis_index("ha"), lax.axis_index("col")
    devs = lax.axis_size("dev")
    chip, core = col // 2, lax.rem(col, 2)
    right = 2 * lax.rem(chip + 1, 4) + core
    left = 2 * lax.rem(chip + 3, 4) + core
    partner = 2 * chip + 1 - core
    up, down = lax.rem(dev + 1, devs), lax.rem(dev + devs - 1, devs)
    other = 1 - ha

    barrier = pltpu.get_barrier_semaphore()
    has_up, has_down = dev < devs - 1, dev > 0
    late = jnp.logical_and(has_down, lax.rem(dev, 8) == 0)
    early = jnp.logical_and(has_up, lax.rem(dev, 8) == 7)
    greets_up = jnp.logical_and(has_up, jnp.logical_not(early))
    prompt = jnp.logical_and(has_down, jnp.logical_not(late))

    def greet(*targets):
        for target in targets:
            pl.semaphore_signal(barrier, inc=1, device_id=target, device_id_type=MESH)

    greet((dev, ha, right), (dev, ha, left), (dev, ha, partner), (dev, other, col))
    pl.when(greets_up)(lambda: greet((up, ha, col), (up, other, col)))
    pl.when(has_down)(lambda: greet((down, ha, col), (down, other, col)))

    mine = chip
    halo_row = 17 * other

    fetch = [pltpu.make_async_copy(x_hbm.at[:, d], x_in.at[:, d], ins.at[d]) for d in range(4)]
    for d in (3, 0, 1, 2):
        fetch[d].start()
    local = pltpu.make_async_copy(x_ref, g.at[mine, core, 1:5, 1:17], local_sem.at[0])
    parameters = [
        pltpu.make_async_copy(k_hbm, k_ref, local_sem.at[1]),
        pltpu.make_async_copy(b_hbm, b_ref, local_sem.at[2]),
    ]
    for copy in parameters:
        copy.start()
    g[:, :, :, pl.ds(17 * ha, 1)] = jnp.zeros((4, 2, 6, 1, 16, 128), jnp.bfloat16)

    @pl.when(jnp.logical_not(has_down))
    def _():
        g[mine, core, 0, halo_row] = jnp.zeros((16, 128), jnp.bfloat16)

    @pl.when(jnp.logical_not(has_up))
    def _():
        g[mine, core, 5, halo_row] = jnp.zeros((16, 128), jnp.bfloat16)

    for d in (3, 0, 1, 2):
        fetch[d].wait()
        for half in range(2):
            rows = slice(half * 8, half * 8 + 8)
            x_ref[d, rows] = jnp.swapaxes(x_in[:, d, rows], 0, 1)
    local.start()
    pl.semaphore_wait(barrier, 4 + 2 * has_up.astype(jnp.int32) + 2 * prompt.astype(jnp.int32))

    @pl.when(early)
    def _():
        for target in ((up, ha, col), (up, other, col)):
            pl.semaphore_signal(ready, inc=1, device_id=target, device_id_type=MESH)

    def remote(src, dst, send, recv, target):
        return pltpu.make_async_remote_copy(
            src_ref=src, dst_ref=dst, send_sem=send, recv_sem=recv,
            device_id=target, device_id_type=MESH,
        )

    edge = 15 * other
    halos = [
        remote(x_ref.at[3], g.at[mine, core, 0, 1:17], hs.at[0], hr.at[0], (up, ha, col)),
        remote(x_ref.at[0], g.at[mine, core, 5, 1:17], hs.at[1], hr.at[1], (down, ha, col)),
        remote(x_ref.at[:, edge], g.at[mine, core, 1:5, 17 * ha], hs.at[2], hr.at[2], (dev, other, col)),
        remote(x_ref.at[3, edge], g.at[mine, core, 0, 17 * ha], hs.at[3], hr.at[3], (up, other, col)),
        remote(x_ref.at[0, edge], g.at[mine, core, 5, 17 * ha], hs.at[4], hr.at[4], (down, other, col)),
    ]
    def part(unit, chips, side=core):
        if unit == 6:
            return g.at[chips, side, :, halo_row]
        return g.at[chips, side, PLANE[unit], 1:17]

    to = {0: has_up, 1: has_down, 2: None, 3: has_up, 4: has_down}
    come = {0: has_down, 1: has_up, 2: None, 3: has_down, 4: has_up}
    exists = {4: has_down, 5: has_up}

    def when(condition, act):
        if condition is None:
            act()
        else:
            pl.when(condition)(act)

    sends = []

    def own_source(unit):
        return x_ref.at[unit] if unit < 4 else part(unit, mine)

    def send(unit, target, send_sems, recv_sems):
        copy = remote(own_source(unit), part(unit, mine), send_sems.at[unit], recv_sems.at[unit], (dev, ha, target))
        when(exists.get(unit), copy.start)
        sends.append((exists.get(unit), copy))

    def send_own(unit):
        if unit == 6:
            for i in (2, 3, 4):
                when(come[i], halos[i].wait_recv)
        if unit in (4, 5):
            when(come[unit - 4], halos[unit - 4].wait_recv)
        if unit != 5:
            send(unit, right, ls, lr)
        if unit != 4:
            send(unit, left, rs, rr)

    def arrival(unit, chips, send, recv, side=core):
        return remote(part(unit, chips, side), part(unit, chips, side), send.at[unit], recv.at[unit], (dev, ha, partner))

    from_left = lax.rem(chip + 3, 4)
    from_right = lax.rem(chip + 1, 4)
    across = lax.rem(chip + 2, 4)

    def relay(unit):
        arrival(unit, from_left, ls, lr).wait_recv()
        arrival(unit, from_right, rs, rr).wait_recv()
        chips, target = (from_left, right) if unit in RELAY_RIGHT else (from_right, left)
        copy = remote(part(unit, chips), part(unit, chips), xs.at[unit], xr.at[unit], (dev, ha, target))
        copy.start()
        sends.append((None, copy))
        if unit == 0:
            when(prompt, to_depth[0].start)
        if unit == 3:
            when(has_up, to_depth[2].start)

    def depth(chips, halo, index):
        plane, target = (4, up) if halo == 0 else (1, down)
        return remote(
            g.at[chips, core, plane, 1:17], g.at[chips, core, halo, 1:17], zs.at[index], zr.at[index], (target, ha, col)
        )

    to_depth = [depth(from_left, 5, 0), depth(across, 5, 1), depth(from_right, 0, 2), depth(across, 0, 3)]
    every = pl.ds(0, 4)

    def forward(unit):
        def whole():
            if unit == 4:
                arrival(unit, from_left, ls, lr).wait_recv()
                to_depth[2].wait_recv()
                to_depth[3].wait_recv()
            elif unit == 5:
                arrival(unit, from_right, rs, rr).wait_recv()
                to_depth[0].wait_recv()
                to_depth[1].wait_recv()
            else:
                arrival(unit, across, xs, xr).wait_recv()

        copy = remote(part(unit, every), part(unit, every), ps.at[unit], pr.at[unit], (dev, ha, partner))
        when(exists.get(unit), whole)
        when(exists.get(unit), copy.start)
        sends.append((exists.get(unit), copy))
        if unit == 0:
            when(prompt, to_depth[1].start)
        if unit == 3:
            when(has_up, to_depth[3].start)

    send_own(ORDER[0])
    for i in (0, 1, 2, 3, 4):
        when(prompt if i in (1, 4) else to[i], halos[i].start)
    send_own(ORDER[1])

    for copy in parameters:
        copy.wait()
    for a in range(3):
        for b in range(3):
            wb[a * 48 : a * 48 + 48, b * 128 : b * 128 + 128] = k_ref[a, b].reshape(48, 128)
    eye = lax.broadcasted_iota(jnp.int32, (16, 16), 0) == lax.broadcasted_iota(jnp.int32, (16, 16), 1)
    bias = jnp.sum(jnp.where(eye, b_ref[...], 0.0), axis=1, keepdims=True)

    seen = set()

    def compute(plane, pairs):
        taps = [a for a in range(3) if 0 <= plane - a < 4]
        low, high = taps[0] * 48, taps[-1] * 48 + 48
        fresh = {a: (plane - a, pairs) not in seen and pairs != "all" for a in taps}
        seen.update((plane - a, pairs) for a in taps)

        def pair(j, carry):
            rows = [g[:, :, plane, 2 * j + i].reshape(128, 128) for i in range(4)]
            cells = jnp.concatenate([jnp.concatenate(rows[i : i + 2], axis=1) for i in range(3)], axis=0)
            out = jnp.dot(wb[low:high, :], cells, preferred_element_type=jnp.float32)
            for a in taps:
                value = out[a * 48 - low : a * 48 - low + 48]
                if fresh[a]:
                    acc[plane - a, j] = value
                else:
                    acc[plane - a, j] += value
            return carry

        if pairs == "inner":
            lax.fori_loop(0, 7, lambda i, carry: pair(ha + i, carry), 0, unroll=7)
        elif pairs == "edge":
            pair(7 * other, 0)
        else:
            lax.fori_loop(0, 8, pair, 0, unroll=4)

    lane = lax.broadcasted_iota(jnp.int32, (16, 128), 1)

    def finish(d):
        def pair(j, carry):
            for half in range(2):
                lanes = slice(half * 128, half * 128 + 128)
                before = pltpu.roll(acc[d, j, 0:16, lanes], 1, 1)
                after = pltpu.roll(acc[d, j, 32:48, lanes], 127, 1)
                total = acc[d, j, 16:32, lanes] + bias
                total += jnp.where(lane == 0, 0.0, before) + jnp.where(lane == 127, 0.0, after)
                o_ref[d, 2 * j + half] = jnp.where(total >= 0, total, 0.3 * total).astype(jnp.bfloat16)
            return carry

        lax.fori_loop(0, 8, pair, 0, unroll=4)
        results[d].start()

    results = [pltpu.make_async_copy(o_ref.at[d], o_hbm.at[d], os.at[d]) for d in range(4)]
    queue = ORDER + TAIL
    steps = len(queue)
    for step in range(steps + 2):
        if step < len(ORDER):
            relay(queue[step])
        if step + 2 < steps:
            send_own(queue[step + 2])
        if 1 <= step <= steps:
            if step == 1:
                local.wait()
            forward(queue[step - 1])
        if step == LATE_STEP:

            @pl.when(late)
            def _():
                pl.semaphore_wait(ready, 2)
                for copy in (halos[4], halos[1], to_depth[0], to_depth[1]):
                    copy.start()

        if step >= 2:
            unit = queue[step - 2]
            when(exists.get(unit), arrival(unit, every, ps, pr, 1 - core).wait_recv)
            if unit < 4:
                compute(PLANE[unit], "inner")
            elif unit == 6:
                for own in ORDER[:4]:
                    compute(PLANE[own], "edge")
                finish(1)
                finish(2)
            else:
                when(exists[unit], lambda: compute(PLANE[unit], "all"))
                finish(0 if unit == 4 else 3)
    for i in range(5):
        when(to[i], halos[i].wait_send)
    for i in range(4):
        when(has_down if i < 2 else has_up, to_depth[i].wait_send)
    for condition, copy in sends:
        when(condition, copy.wait_send)
    for copy in results:
        copy.wait()


def per_device(features, weights, channel_bias):
    dma = pltpu.SemaphoreType.DMA
    out = pl.pallas_call(
        kernel,
        out_shape=jax.ShapeDtypeStruct((4, 16, 16, 128), jnp.bfloat16),
        in_specs=[pl.BlockSpec(memory_space=pl.ANY)] * 3,
        out_specs=pl.BlockSpec(memory_space=pl.ANY),
        scratch_shapes=[
            pltpu.VMEM((4, 2, 6, 18, 16, 128), jnp.bfloat16),
            pltpu.VMEM((144, 384), jnp.bfloat16),
            pltpu.VMEM((4, 8, 48, 256), jnp.float32),
            pltpu.VMEM((3, 3, 3, 16, 128), jnp.bfloat16),
            pltpu.VMEM((1, 16), jnp.float32),
            pltpu.VMEM((4, 16, 16, 128), jnp.bfloat16),
            pltpu.VMEM((16, 4, 16, 128), jnp.bfloat16),
            pltpu.VMEM((4, 16, 16, 128), jnp.bfloat16),
            dma((3,)), dma((4,)), dma((4,)), pltpu.SemaphoreType.REGULAR,
            dma((5,)), dma((5,)),
            dma((7,)), dma((7,)), dma((7,)), dma((7,)),
            dma((7,)), dma((7,)), dma((7,)), dma((7,)),
            dma((4,)), dma((4,)),
        ],
        compiler_params=pltpu.CompilerParams(collective_id=0, has_side_effects=True),
    )(features, weights, channel_bias[None, :])
    return jnp.transpose(out, (2, 0, 1, 3))


def solution(mesh):
    in_specs = (P("col", "dev", "ha", None), P(None, None, None, "col", None), P("col"))
    out_specs = P("col", "dev", "ha", None)
    return jax.shard_map(
        per_device, mesh=mesh, in_specs=in_specs, out_specs=out_specs, check_vma=False
    )
```

```python
import jax
import jax.numpy as jnp
from jax import lax
from jax.experimental import pallas as pl
from jax.experimental.pallas import tpu as pltpu
from jax.sharding import PartitionSpec as P

MESH = pl.DeviceIdType.MESH

ORDER = (3, 0, 1, 2, 6)
TAIL = (4, 5)
LATE_STEP = 2
PLANE = {0: 1, 1: 2, 2: 3, 3: 4, 4: 0, 5: 5}
RELAY_RIGHT = (0, 1, 6)


def kernel(x_hbm, k_hbm, b_hbm, o_hbm, g, wb, acc, k_ref, b_ref, o_ref, y_ref, x_in, x_ref, local_sem, os, ins, ready, hs, hr, ls, lr, rs, rr, xs, xr, ps, pr, zs, zr):
    dev, ha, col = lax.axis_index("dev"), lax.axis_index("ha"), lax.axis_index("col")
    devs = lax.axis_size("dev")
    chip, core = col // 2, lax.rem(col, 2)
    right = 2 * lax.rem(chip + 1, 4) + core
    left = 2 * lax.rem(chip + 3, 4) + core
    partner = 2 * chip + 1 - core
    up, down = lax.rem(dev + 1, devs), lax.rem(dev + devs - 1, devs)
    other = 1 - ha

    barrier = pltpu.get_barrier_semaphore()
    has_up, has_down = dev < devs - 1, dev > 0
    late = jnp.logical_and(has_down, lax.rem(dev, 8) == 0)
    early = jnp.logical_and(has_up, lax.rem(dev, 8) == 7)
    greets_up = jnp.logical_and(has_up, jnp.logical_not(early))
    prompt = jnp.logical_and(has_down, jnp.logical_not(late))

    def greet(*targets):
        for target in targets:
            pl.semaphore_signal(barrier, inc=1, device_id=target, device_id_type=MESH)

    greet((dev, ha, right), (dev, ha, left), (dev, ha, partner), (dev, other, col))
    pl.when(greets_up)(lambda: greet((up, ha, col), (up, other, col)))
    pl.when(has_down)(lambda: greet((down, ha, col), (down, other, col)))

    mine = chip
    halo_row = 17 * other

    fetch = [pltpu.make_async_copy(x_hbm.at[:, d], x_in.at[:, d], ins.at[d]) for d in range(4)]
    for d in (3, 0, 1, 2):
        fetch[d].start()
    local = pltpu.make_async_copy(x_ref, g.at[mine, core, 1:5, 1:17], local_sem.at[0])
    parameters = [
        pltpu.make_async_copy(k_hbm, k_ref, local_sem.at[1]),
        pltpu.make_async_copy(b_hbm, b_ref, local_sem.at[2]),
    ]
    for copy in parameters:
        copy.start()
    g[:, :, :, pl.ds(17 * ha, 1)] = jnp.zeros((4, 2, 6, 1, 16, 128), jnp.bfloat16)

    @pl.when(jnp.logical_not(has_down))
    def _():
        g[mine, core, 0, halo_row] = jnp.zeros((16, 128), jnp.bfloat16)

    @pl.when(jnp.logical_not(has_up))
    def _():
        g[mine, core, 5, halo_row] = jnp.zeros((16, 128), jnp.bfloat16)

    for d in (3, 0, 1, 2):
        fetch[d].wait()
        for half in range(2):
            rows = slice(half * 8, half * 8 + 8)
            x_ref[d, rows] = jnp.swapaxes(x_in[:, d, rows], 0, 1)
    local.start()
    pl.semaphore_wait(barrier, 4 + 2 * has_up.astype(jnp.int32) + 2 * prompt.astype(jnp.int32))

    @pl.when(early)
    def _():
        for target in ((up, ha, col), (up, other, col)):
            pl.semaphore_signal(ready, inc=1, device_id=target, device_id_type=MESH)

    def remote(src, dst, send, recv, target):
        return pltpu.make_async_remote_copy(
            src_ref=src, dst_ref=dst, send_sem=send, recv_sem=recv,
            device_id=target, device_id_type=MESH,
        )

    edge = 15 * other
    halos = [
        remote(x_ref.at[3], g.at[mine, core, 0, 1:17], hs.at[0], hr.at[0], (up, ha, col)),
        remote(x_ref.at[0], g.at[mine, core, 5, 1:17], hs.at[1], hr.at[1], (down, ha, col)),
        remote(x_ref.at[:, edge], g.at[mine, core, 1:5, 17 * ha], hs.at[2], hr.at[2], (dev, other, col)),
        remote(x_ref.at[3, edge], g.at[mine, core, 0, 17 * ha], hs.at[3], hr.at[3], (up, other, col)),
        remote(x_ref.at[0, edge], g.at[mine, core, 5, 17 * ha], hs.at[4], hr.at[4], (down, other, col)),
    ]
    def part(unit, chips, side=core):
        if unit == 6:
            return g.at[chips, side, :, halo_row]
        return g.at[chips, side, PLANE[unit], 1:17]

    to = {0: has_up, 1: has_down, 2: None, 3: has_up, 4: has_down}
    come = {0: has_down, 1: has_up, 2: None, 3: has_down, 4: has_up}
    exists = {4: has_down, 5: has_up}

    def when(condition, act):
        if condition is None:
            act()
        else:
            pl.when(condition)(act)

    sends = []

    def own_source(unit):
        return x_ref.at[unit] if unit < 4 else part(unit, mine)

    def send(unit, target, send_sems, recv_sems):
        copy = remote(own_source(unit), part(unit, mine), send_sems.at[unit], recv_sems.at[unit], (dev, ha, target))
        when(exists.get(unit), copy.start)
        sends.append((exists.get(unit), copy))

    def send_own(unit):
        if unit == 6:
            for i in (2, 3, 4):
                when(come[i], halos[i].wait_recv)
        if unit in (4, 5):
            when(come[unit - 4], halos[unit - 4].wait_recv)
        if unit != 5:
            send(unit, right, ls, lr)
        if unit != 4:
            send(unit, left, rs, rr)

    def arrival(unit, chips, send, recv, side=core):
        return remote(part(unit, chips, side), part(unit, chips, side), send.at[unit], recv.at[unit], (dev, ha, partner))

    from_left = lax.rem(chip + 3, 4)
    from_right = lax.rem(chip + 1, 4)
    across = lax.rem(chip + 2, 4)

    def relay(unit):
        arrival(unit, from_left, ls, lr).wait_recv()
        arrival(unit, from_right, rs, rr).wait_recv()
        chips, target = (from_left, right) if unit in RELAY_RIGHT else (from_right, left)
        copy = remote(part(unit, chips), part(unit, chips), xs.at[unit], xr.at[unit], (dev, ha, target))
        copy.start()
        sends.append((None, copy))
        if unit == 0:
            when(prompt, to_depth[0].start)
        if unit == 3:
            when(has_up, to_depth[2].start)

    def depth(chips, halo, index):
        plane, target = (4, up) if halo == 0 else (1, down)
        return remote(
            g.at[chips, core, plane, 1:17], g.at[chips, core, halo, 1:17], zs.at[index], zr.at[index], (target, ha, col)
        )

    to_depth = [depth(from_left, 5, 0), depth(across, 5, 1), depth(from_right, 0, 2), depth(across, 0, 3)]
    every = pl.ds(0, 4)

    def forward(unit):
        def whole():
            if unit == 4:
                arrival(unit, from_left, ls, lr).wait_recv()
                to_depth[2].wait_recv()
                to_depth[3].wait_recv()
            elif unit == 5:
                arrival(unit, from_right, rs, rr).wait_recv()
                to_depth[0].wait_recv()
                to_depth[1].wait_recv()
            else:
                arrival(unit, across, xs, xr).wait_recv()

        copy = remote(part(unit, every), part(unit, every), ps.at[unit], pr.at[unit], (dev, ha, partner))
        when(exists.get(unit), whole)
        when(exists.get(unit), copy.start)
        sends.append((exists.get(unit), copy))
        if unit == 0:
            when(prompt, to_depth[1].start)
        if unit == 3:
            when(has_up, to_depth[3].start)

    send_own(ORDER[0])
    for i in (0, 1, 2, 3, 4):
        when(prompt if i in (1, 4) else to[i], halos[i].start)
    send_own(ORDER[1])

    for copy in parameters:
        copy.wait()
    for a in range(3):
        for b in range(3):
            wb[a * 48 : a * 48 + 48, b * 128 : b * 128 + 128] = k_ref[a, b].reshape(48, 128)
    eye = lax.broadcasted_iota(jnp.int32, (16, 16), 0) == lax.broadcasted_iota(jnp.int32, (16, 16), 1)
    bias = jnp.sum(jnp.where(eye, b_ref[...], 0.0), axis=1, keepdims=True)

    seen = set()

    def compute(plane, pairs):
        taps = [a for a in range(3) if 0 <= plane - a < 4]
        low, high = taps[0] * 48, taps[-1] * 48 + 48
        fresh = {a: (plane - a, pairs) not in seen and pairs != "all" for a in taps}
        seen.update((plane - a, pairs) for a in taps)

        def pair(j, carry):
            rows = [g[:, :, plane, 2 * j + i].reshape(128, 128) for i in range(4)]
            cells = jnp.concatenate([jnp.concatenate(rows[i : i + 2], axis=1) for i in range(3)], axis=0)
            out = jnp.dot(wb[low:high, :], cells, preferred_element_type=jnp.float32)
            for a in taps:
                value = out[a * 48 - low : a * 48 - low + 48]
                if fresh[a]:
                    acc[plane - a, j] = value
                else:
                    acc[plane - a, j] += value
            return carry

        if pairs == "inner":
            lax.fori_loop(0, 7, lambda i, carry: pair(ha + i, carry), 0, unroll=7)
        elif pairs == "edge":
            pair(7 * other, 0)
        else:
            lax.fori_loop(0, 8, pair, 0, unroll=4)

    lane = lax.broadcasted_iota(jnp.int32, (16, 128), 1)

    def finish(d):
        def pair(j, carry):
            for half in range(2):
                lanes = slice(half * 128, half * 128 + 128)
                before = pltpu.roll(acc[d, j, 0:16, lanes], 1, 1)
                after = pltpu.roll(acc[d, j, 32:48, lanes], 127, 1)
                total = acc[d, j, 16:32, lanes] + bias
                total += jnp.where(lane == 0, 0.0, before) + jnp.where(lane == 127, 0.0, after)
                o_ref[d, 2 * j + half] = jnp.where(total >= 0, total, 0.3 * total).astype(jnp.bfloat16)
            return carry

        lax.fori_loop(0, 8, pair, 0, unroll=4)
        y_ref[:, d] = jnp.swapaxes(o_ref[d], 0, 1)
        results[d].start()

    results = [pltpu.make_async_copy(y_ref.at[:, d], o_hbm.at[:, d], os.at[d]) for d in range(4)]
    queue = ORDER + TAIL
    steps = len(queue)
    for step in range(steps + 2):
        if step < len(ORDER):
            relay(queue[step])
        if step + 2 < steps:
            send_own(queue[step + 2])
        if 1 <= step <= steps:
            if step == 1:
                local.wait()
            forward(queue[step - 1])
        if step == LATE_STEP:

            @pl.when(late)
            def _():
                pl.semaphore_wait(ready, 2)
                for copy in (halos[4], halos[1], to_depth[0], to_depth[1]):
                    copy.start()

        if step >= 2:
            unit = queue[step - 2]
            when(exists.get(unit), arrival(unit, every, ps, pr, 1 - core).wait_recv)
            if unit < 4:
                compute(PLANE[unit], "inner")
            elif unit == 6:
                for own in ORDER[:4]:
                    compute(PLANE[own], "edge")
                finish(1)
                finish(2)
            else:
                when(exists[unit], lambda: compute(PLANE[unit], "all"))
                finish(0 if unit == 4 else 3)
    for i in range(5):
        when(to[i], halos[i].wait_send)
    for i in range(4):
        when(has_down if i < 2 else has_up, to_depth[i].wait_send)
    for condition, copy in sends:
        when(condition, copy.wait_send)
    for copy in results:
        copy.wait()


def per_device(features, weights, channel_bias):
    dma = pltpu.SemaphoreType.DMA
    out = pl.pallas_call(
        kernel,
        out_shape=pltpu.VMEM((16, 4, 16, 128), jnp.bfloat16),
        in_specs=[pl.BlockSpec(memory_space=pl.ANY)] * 3,
        out_specs=pl.BlockSpec(memory_space=pltpu.VMEM),
        scratch_shapes=[
            pltpu.VMEM((4, 2, 6, 18, 16, 128), jnp.bfloat16),
            pltpu.VMEM((144, 384), jnp.bfloat16),
            pltpu.VMEM((4, 8, 48, 256), jnp.float32),
            pltpu.VMEM((3, 3, 3, 16, 128), jnp.bfloat16),
            pltpu.VMEM((1, 16), jnp.float32),
            pltpu.VMEM((4, 16, 16, 128), jnp.bfloat16),
            pltpu.VMEM((16, 4, 16, 128), jnp.bfloat16),
            pltpu.VMEM((16, 4, 16, 128), jnp.bfloat16),
            pltpu.VMEM((4, 16, 16, 128), jnp.bfloat16),
            dma((3,)), dma((4,)), dma((4,)), pltpu.SemaphoreType.REGULAR,
            dma((5,)), dma((5,)),
            dma((7,)), dma((7,)), dma((7,)), dma((7,)),
            dma((7,)), dma((7,)), dma((7,)), dma((7,)),
            dma((4,)), dma((4,)),
        ],
        compiler_params=pltpu.CompilerParams(collective_id=0, has_side_effects=True),
    )(features, weights, channel_bias[None, :])
    return out


def solution(mesh):
    in_specs = (P("col", "dev", "ha", None), P(None, None, None, "col", None), P("col"))
    out_specs = P("col", "dev", "ha", None)
    return jax.shard_map(
        per_device, mesh=mesh, in_specs=in_specs, out_specs=out_specs, check_vma=False
    )
```

```python
import jax
import jax.numpy as jnp
from jax import lax
from jax.experimental import pallas as pl
from jax.experimental.pallas import tpu as pltpu
from jax.sharding import PartitionSpec as P

MESH = pl.DeviceIdType.MESH

ORDER = (3, 0, 1, 2, 6)
TAIL = (4, 5)
LATE_STEP = 2
PLANE = {0: 1, 1: 2, 2: 3, 3: 4, 4: 0, 5: 5}
RELAY_RIGHT = (0, 1, 6)


def kernel(x_hbm, k_hbm, b_hbm, y_ref, g, wb, acc, k_ref, b_ref, o_ref, x_in, x_ref, local_sem, ins, ready, hs, hr, ls, lr, rs, rr, xs, xr, ps, pr, zs, zr):
    dev, ha, col = lax.axis_index("dev"), lax.axis_index("ha"), lax.axis_index("col")
    devs = lax.axis_size("dev")
    chip, core = col // 2, lax.rem(col, 2)
    right = 2 * lax.rem(chip + 1, 4) + core
    left = 2 * lax.rem(chip + 3, 4) + core
    partner = 2 * chip + 1 - core
    up, down = lax.rem(dev + 1, devs), lax.rem(dev + devs - 1, devs)
    other = 1 - ha

    barrier = pltpu.get_barrier_semaphore()
    has_up, has_down = dev < devs - 1, dev > 0
    late = jnp.logical_and(has_down, lax.rem(dev, 8) == 0)
    early = jnp.logical_and(has_up, lax.rem(dev, 8) == 7)
    greets_up = jnp.logical_and(has_up, jnp.logical_not(early))
    prompt = jnp.logical_and(has_down, jnp.logical_not(late))

    def greet(*targets):
        for target in targets:
            pl.semaphore_signal(barrier, inc=1, device_id=target, device_id_type=MESH)

    greet((dev, ha, right), (dev, ha, left), (dev, ha, partner), (dev, other, col))
    pl.when(greets_up)(lambda: greet((up, ha, col), (up, other, col)))
    pl.when(has_down)(lambda: greet((down, ha, col), (down, other, col)))

    mine = chip
    halo_row = 17 * other

    fetch = [pltpu.make_async_copy(x_hbm.at[:, d], x_in.at[:, d], ins.at[d]) for d in range(4)]
    for d in (3, 0, 1, 2):
        fetch[d].start()
    local = pltpu.make_async_copy(x_ref, g.at[mine, core, 1:5, 1:17], local_sem.at[0])
    parameters = [
        pltpu.make_async_copy(k_hbm, k_ref, local_sem.at[1]),
        pltpu.make_async_copy(b_hbm, b_ref, local_sem.at[2]),
    ]
    for copy in parameters:
        copy.start()
    g[:, :, :, pl.ds(17 * ha, 1)] = jnp.zeros((4, 2, 6, 1, 16, 128), jnp.bfloat16)

    @pl.when(jnp.logical_not(has_down))
    def _():
        g[mine, core, 0, halo_row] = jnp.zeros((16, 128), jnp.bfloat16)

    @pl.when(jnp.logical_not(has_up))
    def _():
        g[mine, core, 5, halo_row] = jnp.zeros((16, 128), jnp.bfloat16)

    for d in (3, 0, 1, 2):
        fetch[d].wait()
        for half in range(2):
            rows = slice(half * 8, half * 8 + 8)
            x_ref[d, rows] = jnp.swapaxes(x_in[:, d, rows], 0, 1)
    local.start()
    pl.semaphore_wait(barrier, 4 + 2 * has_up.astype(jnp.int32) + 2 * prompt.astype(jnp.int32))

    @pl.when(early)
    def _():
        for target in ((up, ha, col), (up, other, col)):
            pl.semaphore_signal(ready, inc=1, device_id=target, device_id_type=MESH)

    def remote(src, dst, send, recv, target):
        return pltpu.make_async_remote_copy(
            src_ref=src, dst_ref=dst, send_sem=send, recv_sem=recv,
            device_id=target, device_id_type=MESH,
        )

    edge = 15 * other
    halos = [
        remote(x_ref.at[3], g.at[mine, core, 0, 1:17], hs.at[0], hr.at[0], (up, ha, col)),
        remote(x_ref.at[0], g.at[mine, core, 5, 1:17], hs.at[1], hr.at[1], (down, ha, col)),
        remote(x_ref.at[:, edge], g.at[mine, core, 1:5, 17 * ha], hs.at[2], hr.at[2], (dev, other, col)),
        remote(x_ref.at[3, edge], g.at[mine, core, 0, 17 * ha], hs.at[3], hr.at[3], (up, other, col)),
        remote(x_ref.at[0, edge], g.at[mine, core, 5, 17 * ha], hs.at[4], hr.at[4], (down, other, col)),
    ]
    def part(unit, chips, side=core):
        if unit == 6:
            return g.at[chips, side, :, halo_row]
        return g.at[chips, side, PLANE[unit], 1:17]

    to = {0: has_up, 1: has_down, 2: None, 3: has_up, 4: has_down}
    come = {0: has_down, 1: has_up, 2: None, 3: has_down, 4: has_up}
    exists = {4: has_down, 5: has_up}

    def when(condition, act):
        if condition is None:
            act()
        else:
            pl.when(condition)(act)

    sends = []

    def own_source(unit):
        return x_ref.at[unit] if unit < 4 else part(unit, mine)

    def send(unit, target, send_sems, recv_sems):
        copy = remote(own_source(unit), part(unit, mine), send_sems.at[unit], recv_sems.at[unit], (dev, ha, target))
        when(exists.get(unit), copy.start)
        sends.append((exists.get(unit), copy))

    def send_own(unit):
        if unit == 6:
            for i in (2, 3, 4):
                when(come[i], halos[i].wait_recv)
        if unit in (4, 5):
            when(come[unit - 4], halos[unit - 4].wait_recv)
        if unit != 5:
            send(unit, right, ls, lr)
        if unit != 4:
            send(unit, left, rs, rr)

    def arrival(unit, chips, send, recv, side=core):
        return remote(part(unit, chips, side), part(unit, chips, side), send.at[unit], recv.at[unit], (dev, ha, partner))

    from_left = lax.rem(chip + 3, 4)
    from_right = lax.rem(chip + 1, 4)
    across = lax.rem(chip + 2, 4)

    def relay(unit):
        arrival(unit, from_left, ls, lr).wait_recv()
        arrival(unit, from_right, rs, rr).wait_recv()
        chips, target = (from_left, right) if unit in RELAY_RIGHT else (from_right, left)
        copy = remote(part(unit, chips), part(unit, chips), xs.at[unit], xr.at[unit], (dev, ha, target))
        copy.start()
        sends.append((None, copy))
        if unit == 0:
            when(prompt, to_depth[0].start)
        if unit == 3:
            when(has_up, to_depth[2].start)

    def depth(chips, halo, index):
        plane, target = (4, up) if halo == 0 else (1, down)
        return remote(
            g.at[chips, core, plane, 1:17], g.at[chips, core, halo, 1:17], zs.at[index], zr.at[index], (target, ha, col)
        )

    to_depth = [depth(from_left, 5, 0), depth(across, 5, 1), depth(from_right, 0, 2), depth(across, 0, 3)]
    every = pl.ds(0, 4)

    def forward(unit):
        def whole():
            if unit == 4:
                arrival(unit, from_left, ls, lr).wait_recv()
                to_depth[2].wait_recv()
                to_depth[3].wait_recv()
            elif unit == 5:
                arrival(unit, from_right, rs, rr).wait_recv()
                to_depth[0].wait_recv()
                to_depth[1].wait_recv()
            else:
                arrival(unit, across, xs, xr).wait_recv()

        copy = remote(part(unit, every), part(unit, every), ps.at[unit], pr.at[unit], (dev, ha, partner))
        when(exists.get(unit), whole)
        when(exists.get(unit), copy.start)
        sends.append((exists.get(unit), copy))
        if unit == 0:
            when(prompt, to_depth[1].start)
        if unit == 3:
            when(has_up, to_depth[3].start)

    send_own(ORDER[0])
    for i in (0, 1, 2, 3, 4):
        when(prompt if i in (1, 4) else to[i], halos[i].start)
    send_own(ORDER[1])

    for copy in parameters:
        copy.wait()
    for a in range(3):
        for b in range(3):
            wb[a * 48 : a * 48 + 48, b * 128 : b * 128 + 128] = k_ref[a, b].reshape(48, 128)
    eye = lax.broadcasted_iota(jnp.int32, (16, 16), 0) == lax.broadcasted_iota(jnp.int32, (16, 16), 1)
    bias = jnp.sum(jnp.where(eye, b_ref[...], 0.0), axis=1, keepdims=True)

    seen = set()

    def compute(plane, pairs):
        taps = [a for a in range(3) if 0 <= plane - a < 4]
        low, high = taps[0] * 48, taps[-1] * 48 + 48
        fresh = {a: (plane - a, pairs) not in seen and pairs != "all" for a in taps}
        seen.update((plane - a, pairs) for a in taps)

        def pair(j, carry):
            rows = [g[:, :, plane, 2 * j + i].reshape(128, 128) for i in range(4)]
            cells = jnp.concatenate([jnp.concatenate(rows[i : i + 2], axis=1) for i in range(3)], axis=0)
            out = jnp.dot(wb[low:high, :], cells, preferred_element_type=jnp.float32)
            for a in taps:
                value = out[a * 48 - low : a * 48 - low + 48]
                if fresh[a]:
                    acc[plane - a, j] = value
                else:
                    acc[plane - a, j] += value
            return carry

        if pairs == "inner":
            lax.fori_loop(0, 7, lambda i, carry: pair(ha + i, carry), 0, unroll=7)
        elif pairs == "edge":
            pair(7 * other, 0)
        else:
            lax.fori_loop(0, 8, pair, 0, unroll=4)

    lane = lax.broadcasted_iota(jnp.int32, (16, 128), 1)

    def finish(d):
        def pair(j, carry):
            for half in range(2):
                lanes = slice(half * 128, half * 128 + 128)
                before = pltpu.roll(acc[d, j, 0:16, lanes], 1, 1)
                after = pltpu.roll(acc[d, j, 32:48, lanes], 127, 1)
                total = acc[d, j, 16:32, lanes] + bias
                total += jnp.where(lane == 0, 0.0, before) + jnp.where(lane == 127, 0.0, after)
                o_ref[d, 2 * j + half] = jnp.where(total >= 0, total, 0.3 * total).astype(jnp.bfloat16)
            return carry

        lax.fori_loop(0, 8, pair, 0, unroll=4)
        y_ref[:, d] = jnp.swapaxes(o_ref[d], 0, 1)

    queue = ORDER + TAIL
    steps = len(queue)
    for step in range(steps + 2):
        if step < len(ORDER):
            relay(queue[step])
        if step + 2 < steps:
            send_own(queue[step + 2])
        if 1 <= step <= steps:
            if step == 1:
                local.wait()
            forward(queue[step - 1])
        if step == LATE_STEP:

            @pl.when(late)
            def _():
                pl.semaphore_wait(ready, 2)
                for copy in (halos[4], halos[1], to_depth[0], to_depth[1]):
                    copy.start()

        if step >= 2:
            unit = queue[step - 2]
            when(exists.get(unit), arrival(unit, every, ps, pr, 1 - core).wait_recv)
            if unit < 4:
                compute(PLANE[unit], "inner")
            elif unit == 6:
                for own in ORDER[:4]:
                    compute(PLANE[own], "edge")
                finish(1)
                finish(2)
            else:
                when(exists[unit], lambda: compute(PLANE[unit], "all"))
                finish(0 if unit == 4 else 3)
    for i in range(5):
        when(to[i], halos[i].wait_send)
    for i in range(4):
        when(has_down if i < 2 else has_up, to_depth[i].wait_send)
    for condition, copy in sends:
        when(condition, copy.wait_send)


def per_device(features, weights, channel_bias):
    dma = pltpu.SemaphoreType.DMA
    out = pl.pallas_call(
        kernel,
        out_shape=pltpu.VMEM((16, 4, 16, 128), jnp.bfloat16),
        in_specs=[pl.BlockSpec(memory_space=pl.ANY)] * 3,
        out_specs=pl.BlockSpec(memory_space=pltpu.VMEM),
        scratch_shapes=[
            pltpu.VMEM((4, 2, 6, 18, 16, 128), jnp.bfloat16),
            pltpu.VMEM((144, 384), jnp.bfloat16),
            pltpu.VMEM((4, 8, 48, 256), jnp.float32),
            pltpu.VMEM((3, 3, 3, 16, 128), jnp.bfloat16),
            pltpu.VMEM((1, 16), jnp.float32),
            pltpu.VMEM((4, 16, 16, 128), jnp.bfloat16),
            pltpu.VMEM((16, 4, 16, 128), jnp.bfloat16),
            pltpu.VMEM((4, 16, 16, 128), jnp.bfloat16),
            dma((3,)), dma((4,)), pltpu.SemaphoreType.REGULAR,
            dma((5,)), dma((5,)),
            dma((7,)), dma((7,)), dma((7,)), dma((7,)),
            dma((7,)), dma((7,)), dma((7,)), dma((7,)),
            dma((4,)), dma((4,)),
        ],
        compiler_params=pltpu.CompilerParams(collective_id=0, has_side_effects=True),
    )(features, weights, channel_bias[None, :])
    return out


def solution(mesh):
    in_specs = (P("col", "dev", "ha", None), P(None, None, None, "col", None), P("col"))
    out_specs = P("col", "dev", "ha", None)
    return jax.shard_map(
        per_device, mesh=mesh, in_specs=in_specs, out_specs=out_specs, check_vma=False
    )
```
